32 devices in a mesh: section: 8 (over y, x, core), shard: 4 (over z).
Axes of the slice: x: 2, y: 2, z: 4, core: 2. Of those that a mesh axis runs over, the one named last changes fastest.
Arguments:
- kept_slab: bfloat16 [131072, 768], P(('section', 'shard')), may hold values from -1 to 1, as said below
- new_rows: bfloat16 [4, 256, 768], P(None, ('section', 'shard')), may hold values from -1 to 1, as said below
- append_mask: int32 [4, 256], P(None, ('section', 'shard')), may hold values 0 or 1
Outputs:
- maxima: float32 [4, 256], P(None, ('section', 'shard'))
The draws below stay inside these ranges and needn't reach their ends.
Inputs may be any that keep to these rules, and one draw needn't show every extreme that they name: `kept_slab`: every row has unit Euclidean length up to bfloat16 rounding. `new_rows`: every row has unit Euclidean length up to bfloat16 rounding.
All inputs are finite; a program needn't handle non-finite values. No bound on the sum of `append_mask` on one device may be relied on, other than what follows from the above.
Results may differ from the reference program's by a relative error of at most 0.0003.
Values may be sent and summed in bfloat16 or wider, within the bound.
No kernel may reach another device: no remote copies, remote signals or barrier semaphores. Data moves between devices by JAX's collectives and lax.ppermute only.
A program may use at most 64 MiB of HBM per device.

```python
import jax
import jax.numpy as jnp
from jax import lax

D = 768
ROWS_DEV = 4096
MB = 4
BATCH = 256
N_SECTION = 8
N_SHARD = 4


def unit_vector(base_key, index):
    row_key = jax.random.fold_in(base_key, index)
    vector = jax.random.normal(row_key, (D,), jnp.float32)
    return vector / jnp.sqrt(jnp.sum(vector * vector))


def kept_rows_at(key, indices):
    base_key = jax.random.fold_in(key, 11)
    return jax.vmap(lambda index: unit_vector(base_key, index))(indices)


def draw_kept_slab(key, part):
    indices = jnp.arange(ROWS_DEV * N_SECTION * N_SHARD, dtype=jnp.int32)
    return kept_rows_at(key, indices).astype(jnp.bfloat16)


def draw_new_rows(key, part):
    total = MB * BATCH
    own_key = jax.random.fold_in(key, 23)
    subkeys = jax.random.split(own_key, 5)
    sources = jax.random.randint(subkeys[0], (total,), 0, ROWS_DEV * N_SECTION * N_SHARD)
    copies = kept_rows_at(key, sources)
    group_index = jnp.arange(total, dtype=jnp.int32) // BATCH
    earlier = jax.random.randint(subkeys[1], (total,), 0, jnp.maximum(group_index, 1) * BATCH)
    share = jax.random.uniform(subkeys[2], (total,), jnp.float32, 0.2, 1.0)
    linked = jax.random.uniform(subkeys[3], (total,), jnp.float32, 0.5, 2.0)
    linked = jnp.where(group_index > 0, linked, 0.0)
    noise = jax.random.normal(subkeys[4], (total, D), jnp.float32) / jnp.sqrt(jnp.float32(D))
    mixed = share[:, None] * copies + linked[:, None] * noise[earlier] + noise
    mixed = mixed / jnp.sqrt(jnp.sum(mixed * mixed, axis=1, keepdims=True))
    return mixed.reshape(MB, BATCH, D).astype(jnp.bfloat16)


def with_ends(result, stream_key, smallest, high):
    place = [jax.random.randint(jax.random.fold_in(stream_key, axis), (), 0, length) for axis, length in enumerate(result.shape)]
    widest = result.shape.index(max(result.shape))
    neighbour = place[:widest] + [(place[widest] + 1) % result.shape[widest]] + place[widest + 1:]
    return result.at[tuple(place)].set(smallest).at[tuple(neighbour)].set(high)


def setup_inputs(seed: int = 0) -> dict:
    arg_keys = jax.random.split(jax.random.key(seed), 4)
    return {
        "kept_slab": draw_kept_slab(jax.random.fold_in(arg_keys[3], 71), 0),
        "new_rows": draw_new_rows(jax.random.fold_in(arg_keys[3], 71), 0),
        "append_mask": with_ends((jax.random.randint(arg_keys[2], (MB, BATCH), 0, 2) < 1).astype(jnp.int32), jax.random.fold_in(arg_keys[2], 1), 0, 1),
    }


def reference(kept_slab, new_rows, append_mask):
    flattened = new_rows.reshape(MB * BATCH, D)
    blocks = kept_slab.reshape(N_SECTION * N_SHARD, ROWS_DEV, D)

    def visit(highest, block):
        scores = lax.dot_general(flattened, block, (((1,), (1,)), ((), ())), preferred_element_type=jnp.float32)
        return jnp.maximum(highest, jnp.max(scores, axis=1)), None

    slab_best, _ = lax.scan(visit, jnp.full((MB * BATCH,), -3.0, jnp.float32), blocks)
    cross = lax.dot_general(flattened, flattened, (((1,), (1,)), ((), ())), preferred_element_type=jnp.float32)
    groups_of = jnp.arange(MB * BATCH, dtype=jnp.int32) // BATCH
    usable = (groups_of[None, :] < groups_of[:, None]) & (append_mask.reshape(-1)[None, :] == 1)
    stream_best = jnp.max(jnp.where(usable, cross, jnp.float32(-3.0)), axis=1)
    return jnp.maximum(slab_best, stream_best).reshape(MB, BATCH)
```

```python
import functools

import jax
import jax.numpy as jnp
from jax import lax
from jax.experimental import pallas as pl
from jax.experimental.pallas import tpu as pltpu
from jax.sharding import PartitionSpec as P

AXES = ("section", "shard")
LANES = 128
NONE_YET = -3.0


def partner_mask(mesh):
    columns = mesh.shape["shard"]
    devices = mesh.devices
    here, beside = devices[0, 0], devices[0, 1 % columns]
    if columns > 1 and getattr(here, "coords", 0) == getattr(beside, "coords", 1):
        return 1
    return columns


def masks_of(mesh):
    columns, total = mesh.shape["shard"], mesh.size
    pair = partner_mask(mesh)
    inner = [m for m in range(1, columns) if not m & pair]
    outer = [m for m in range(columns, total, columns) if not m & pair]
    return pair, inner, outer


def swap(rows, mask, total):
    return lax.ppermute(rows, AXES, [(i, i ^ mask) for i in range(total)])


def best_of(kept_ref, own_ref, flag_ref, queries, micro_count, own_count):
    count = queries.shape[0]
    contract = (((1,), (1,)), ((), ()))
    tile = min(512, kept_ref.shape[0])
    best = jnp.full((8, count), NONE_YET, jnp.float32)
    for start in range(0, kept_ref.shape[0], tile):
        scores = lax.dot_general(
            kept_ref[start : start + tile, :], queries, contract, preferred_element_type=jnp.float32
        )
        best = jnp.maximum(best, jnp.max(scores.reshape(tile // 8, 8, count), axis=0))
    block = micro_count * own_count
    cross = lax.dot_general(own_ref[...], queries, contract, preferred_element_type=jnp.float32)
    row = lax.broadcasted_iota(jnp.int32, (block, count), 0)
    column = lax.broadcasted_iota(jnp.int32, (block, count), 1)
    earlier = row // own_count < (column % block) // own_count
    usable = earlier & (flag_ref[...] == 1)
    cross = jnp.where(usable, cross, NONE_YET)
    best = jnp.maximum(best, jnp.max(cross.reshape(block // 8, 8, count), axis=0))
    return jnp.max(best, axis=0, keepdims=True)


def chunk_kernel(parts, micro_count, own_count, kept_ref, own_ref, flag_ref, *refs):
    queries = jnp.concatenate([r[...] for r in refs[:parts]], axis=0)
    refs[parts][...] = best_of(kept_ref, own_ref, flag_ref, queries, micro_count, own_count)


def last_kernel(parts, masks, micro_count, own_count, kept_ref, own_ref, flag_ref, *refs):
    queries = jnp.concatenate([r[...] for r in refs[:parts]], axis=0)
    *earlier, out_ref = refs[parts:]
    block = micro_count * own_count
    me = lax.axis_index(AXES[0]) * lax.axis_size(AXES[1]) + lax.axis_index(AXES[1])
    last = best_of(kept_ref, own_ref, flag_ref, queries, micro_count, own_count)
    for best, owners in zip([r[...] for r in earlier] + [last], masks, strict=True):
        short = -best.shape[1] % LANES
        if short:
            best = jnp.concatenate([best, jnp.zeros((1, short), best.dtype)], axis=1)
        for at, mask in enumerate(owners):
            start = at * block
            base = start // LANES * LANES
            piece = best[:, base : base + LANES]
            if start - base:
                piece = pltpu.roll(piece, LANES - (start - base), 1)
            out_ref[jnp.bitwise_xor(me, mask)] = piece


def per_device(mesh, kept_slab, new_rows, append_mask):
    micro_count, own_count, width = new_rows.shape
    block = micro_count * own_count
    total = mesh.size
    pair, inner, outer = masks_of(mesh)
    own = new_rows.reshape(block, width)
    flags = append_mask.reshape(block, 1)
    shared = (kept_slab, own, flags)
    vmem = pl.BlockSpec(memory_space=pltpu.VMEM)

    def params(rows):
        return dict(
            compiler_params=pltpu.CompilerParams(vmem_limit_bytes=24 * 2**20),
            cost_estimate=pl.CostEstimate(
                flops=2 * rows * kept_slab.shape[0] * width,
                bytes_accessed=2 * kept_slab.shape[0] * width,
                transcendentals=0,
            ),
        )

    def chunk(*parts):
        rows = sum(p.shape[0] for p in parts)
        return pl.pallas_call(
            functools.partial(chunk_kernel, len(parts), micro_count, own_count),
            out_shape=jax.ShapeDtypeStruct((1, rows), jnp.float32),
            in_specs=[vmem] * (3 + len(parts)),
            out_specs=vmem,
            **params(rows),
        )(*shared, *parts)

    def last(parts, bests, masks):
        rows = sum(p.shape[0] for p in parts)
        return pl.pallas_call(
            functools.partial(last_kernel, len(parts), masks, micro_count, own_count),
            out_shape=jax.ShapeDtypeStruct((total, 1, LANES), jnp.float32),
            in_specs=[vmem] * (3 + len(parts) + len(bests)),
            out_specs=vmem,
            **params(rows),
        )(*shared, *parts, *bests)

    z = [swap(own, m, total) for m in inner]
    p = [swap(own, m, total) for m in outer]
    z_all = jnp.concatenate(z, axis=0)
    near = [0, *outer, *inner]
    near_all = jnp.concatenate([own, *p, *z], axis=0)
    near_pair = swap(near_all, pair, total)
    far = [swap(z_all, m, total) for m in outer]
    far_pair = [swap(f, pair, total) for f in far]

    bests, masks = [], []
    bests.append(chunk(near_all))
    masks.append(near)
    bests.append(chunk(near_pair))
    masks.append([m ^ pair for m in near])
    far_masks = [[o ^ i for i in inner] for o in outer]
    for mine, theirs, owners in zip(far[:-1], far_pair[:-1], far_masks[:-1], strict=True):
        bests.append(chunk(mine, theirs))
        masks.append(owners + [m ^ pair for m in owners])
    masks.append(far_masks[-1] + [m ^ pair for m in far_masks[-1]])
    partial = last([far[-1], far_pair[-1]], bests, masks)
    received = lax.all_to_all(partial, AXES, split_axis=0, concat_axis=0, tiled=True)
    return jnp.max(received[:, 0, :block], axis=0).reshape(micro_count, own_count)


def solution(mesh):
    return jax.shard_map(
        functools.partial(per_device, mesh),
        mesh=mesh,
        in_specs=(
            P(AXES, None),
            P(None, AXES, None),
            P(None, AXES),
        ),
        out_specs=P(None, AXES),
        check_vma=False,
    )
```

```python
import functools

import jax
import jax.numpy as jnp
from jax import lax
from jax.experimental import pallas as pl
from jax.experimental.pallas import tpu as pltpu
from jax.sharding import PartitionSpec as P

AXES = ("section", "shard")
LANES = 128
CHUNK_ROWS = 256
JOIN_FLOPS = 4_000_000_000
NONE_YET = -3.0


def partner_mask(mesh):
    columns = mesh.shape["shard"]
    devices = mesh.devices
    here, beside = devices[0, 0], devices[0, 1 % columns]
    if columns > 1 and getattr(here, "coords", 0) == getattr(beside, "coords", 1):
        return 1
    return columns


def masks_of(mesh):
    columns, total = mesh.shape["shard"], mesh.size
    pair = partner_mask(mesh)
    near, *inner = [m for m in range(1, columns) if not m & pair]
    outer = [m for m in range(columns, total, columns) if not m & pair]
    return pair, near, inner, outer


def swap(rows, mask, total):
    return lax.ppermute(rows, AXES, [(i, i ^ mask) for i in range(total)])


def join_kernel(*refs):
    *blocks, out_ref = refs
    at = 0
    for block in blocks:
        rows = block.shape[0]
        out_ref[at : at + rows, :] = block[...]
        at += rows


def best_of(kept_ref, own_ref, flag_ref, queries, micro_count, own_count):
    count = queries.shape[0]
    contract = (((1,), (1,)), ((), ()))
    block = micro_count * own_count
    cross = lax.dot_general(own_ref[...], queries, contract, preferred_element_type=jnp.float32)
    row = lax.broadcasted_iota(jnp.int32, (block, count), 0)
    column = lax.broadcasted_iota(jnp.int32, (block, count), 1)
    earlier = row // own_count < (column % block) // own_count
    usable = earlier & (flag_column(flag_ref) == 1)
    cross = jnp.where(usable, cross, NONE_YET)
    best = jnp.max(cross.reshape(block // 8, 8, count), axis=0)
    tile = min(512, kept_ref.shape[0])
    for start in range(0, kept_ref.shape[0], tile):
        scores = lax.dot_general(
            kept_ref[start : start + tile, :], queries, contract, preferred_element_type=jnp.float32
        )
        best = jnp.maximum(best, jnp.max(scores.reshape(tile // 8, 8, count), axis=0))
    return jnp.max(best, axis=0, keepdims=True)


def flag_column(flag_ref):
    groups, count = flag_ref.shape
    row = lax.broadcasted_iota(jnp.int32, (count, count), 0)
    diagonal = row == lax.broadcasted_iota(jnp.int32, (count, count), 1)
    columns = []
    for n in range(groups):
        spread = jnp.broadcast_to(flag_ref[n : n + 1, :], (count, count))
        columns.append(jnp.sum(jnp.where(diagonal, spread, 0), axis=1, keepdims=True))
    return jnp.concatenate(columns, axis=0)


def gathered(refs, spans):
    return jnp.concatenate([r[a:b, :] for r, (a, b) in zip(refs, spans, strict=True)], axis=0)


def chunk_kernel(spans, micro_count, own_count, kept_ref, own_ref, flag_ref, *refs):
    parts = len(spans)
    queries = gathered(refs[:parts], spans)
    refs[parts][...] = best_of(kept_ref, own_ref, flag_ref, queries, micro_count, own_count)


def last_kernel(spans, masks, micro_count, own_count, kept_ref, own_ref, flag_ref, *refs):
    parts = len(spans)
    queries = gathered(refs[:parts], spans)
    *earlier, out_ref = refs[parts:]
    block = micro_count * own_count
    me = lax.axis_index(AXES[0]) * lax.axis_size(AXES[1]) + lax.axis_index(AXES[1])

    def place(best, owners):
        short = -best.shape[1] % LANES
        if short:
            best = jnp.concatenate([best, jnp.zeros((1, short), best.dtype)], axis=1)
        for at, mask in enumerate(owners):
            start = at * block
            base = start // LANES * LANES
            piece = best[:, base : base + LANES]
            if start - base:
                piece = pltpu.roll(piece, LANES - (start - base), 1)
            out_ref[jnp.bitwise_xor(me, mask)] = piece

    for ref, owners in zip(earlier, masks[:-1], strict=True):
        place(ref[...], owners)
    place(best_of(kept_ref, own_ref, flag_ref, queries, micro_count, own_count), masks[-1])


def pack(pieces, block):
    room = CHUNK_ROWS // block
    chunks, spans, owners = [], [], []
    for array, masks in pieces:
        at = 0
        while at < len(masks):
            take = min(room - len(owners), len(masks) - at)
            spans.append((array, at * block, (at + take) * block))
            owners += masks[at : at + take]
            at += take
            if len(owners) == room:
                chunks.append((spans, owners))
                spans, owners = [], []
    if owners:
        chunks.append((spans, owners))
    return chunks


def per_device(mesh, kept_slab, new_rows, append_mask):
    micro_count, own_count, width = new_rows.shape
    block = micro_count * own_count
    total = mesh.size
    pair, near, inner, outer = masks_of(mesh)
    own = new_rows.reshape(block, width)
    slab_rows = kept_slab.shape[0]
    vmem = pl.BlockSpec(memory_space=pltpu.VMEM)
    small = pltpu.CompilerParams(vmem_limit_bytes=8 * 2**20)
    large = pltpu.CompilerParams(vmem_limit_bytes=24 * 2**20)

    def join(*blocks):
        rows = sum(b.shape[0] for b in blocks)
        return pl.pallas_call(
            join_kernel,
            out_shape=jax.ShapeDtypeStruct((rows, width), own.dtype),
            in_specs=[vmem] * len(blocks),
            out_specs=vmem,
            compiler_params=small,
            cost_estimate=pl.CostEstimate(
                flops=JOIN_FLOPS, bytes_accessed=4 * rows * width, transcendentals=0
            ),
        )(*blocks)

    def chunk(spans, owners, bests=(), masks=()):
        rows = len(owners) * block
        cuts = [(a, b) for _, a, b in spans]
        best = jax.ShapeDtypeStruct((1, rows), jnp.float32)
        if masks:
            body = functools.partial(last_kernel, cuts, masks)
            out = jax.ShapeDtypeStruct((total, 1, LANES), jnp.float32)
        else:
            body, out = functools.partial(chunk_kernel, cuts), best
        return pl.pallas_call(
            functools.partial(body, micro_count, own_count),
            out_shape=out,
            in_specs=[vmem] * (3 + len(spans) + len(bests)),
            out_specs=vmem,
            compiler_params=large,
            cost_estimate=pl.CostEstimate(
                flops=2 * rows * slab_rows * width,
                bytes_accessed=2 * slab_rows * width,
                transcendentals=0,
            ),
        )(kept_slab, own, append_mask, *[s[0] for s in spans], *bests)

    z = [swap(own, m, total) for m in inner]
    p = [swap(own, m, total) for m in outer]
    line = join(*z)
    far = [swap(line, m, total) for m in outer]
    side = join(own, *p[:-1])
    beside = [swap(side, near, total), swap(p[-1], near, total)]
    first = join(side, p[-1], line, far[0])
    first_pair = swap(first, pair, total)
    rest = join(*far[1:], *beside)
    rest_pair = swap(rest, pair, total)

    planes = [0, *outer]
    far_masks = [[o ^ i for i in inner] for o in outer]
    first_masks = planes + inner + far_masks[0]
    rest_masks = sum(far_masks[1:], []) + [near ^ m for m in planes]
    pieces = [(first, first_masks), (first_pair, [m ^ pair for m in first_masks])]
    pieces += [(rest, rest_masks), (rest_pair, [m ^ pair for m in rest_masks])]
    chunks = pack(pieces, block)
    bests = [chunk(*c) for c in chunks[:-1]]
    partial = chunk(*chunks[-1], bests, [owners for _, owners in chunks])
    received = lax.all_to_all(partial, AXES, split_axis=0, concat_axis=0, tiled=True)
    return jnp.max(received[:, 0, :block], axis=0).reshape(micro_count, own_count)


def solution(mesh):
    def body(kept_slab, new_rows, append_mask):
        return per_device(mesh, kept_slab, new_rows, append_mask)

    return jax.shard_map(
        body,
        mesh=mesh,
        in_specs=(
            P(AXES, None),
            P(None, AXES, None),
            P(None, AXES),
        ),
        out_specs=P(None, AXES),
        check_vma=False,
    )
```

```python
import functools

import jax
import jax.numpy as jnp
from jax import lax
from jax.experimental import pallas as pl
from jax.experimental.pallas import tpu as pltpu
from jax.sharding import PartitionSpec as P

AXES = ("section", "shard")
LANES = 128
CHUNK_ROWS = 256
JOIN_FLOPS = 4_000_000_000
NONE_YET = -3.0


def partner_mask(mesh):
    columns = mesh.shape["shard"]
    devices = mesh.devices
    here, beside = devices[0, 0], devices[0, 1 % columns]
    if columns > 1 and getattr(here, "coords", 0) == getattr(beside, "coords", 1):
        return 1
    return columns


def masks_of(mesh):
    columns, total = mesh.shape["shard"], mesh.size
    pair = partner_mask(mesh)
    near, *inner = [m for m in range(1, columns) if not m & pair]
    outer = [m for m in range(columns, total, columns) if not m & pair]
    return pair, near, inner, outer


def swap(rows, mask, total, pair=0, other=None):
    second = mask if other is None else other
    return lax.ppermute(rows, AXES, [(i, i ^ (second if i & pair else mask)) for i in range(total)])


def twin_kernel(own_ref, other_ref, out_ref, sem):
    rows = own_ref.shape[0]
    copy = pltpu.make_async_copy(own_ref, out_ref.at[pl.ds(0, rows)], sem)
    copy.start()
    out_ref[rows : 2 * rows, :] = other_ref[...]
    copy.wait()


def join_kernel(*refs):
    *blocks, out_ref = refs
    at = 0
    for block in blocks:
        rows = block.shape[0]
        out_ref[at : at + rows, :] = block[...]
        at += rows


def best_of(kept_ref, own_ref, flag_ref, queries, micro_count, own_count):
    count = queries.shape[0]
    contract = (((1,), (1,)), ((), ()))
    block = micro_count * own_count
    cross = lax.dot_general(own_ref[...], queries, contract, preferred_element_type=jnp.float32)
    row = lax.broadcasted_iota(jnp.int32, (block, count), 0)
    column = lax.broadcasted_iota(jnp.int32, (block, count), 1)
    earlier = row // own_count < (column % block) // own_count
    usable = earlier & (flag_column(flag_ref) == 1)
    cross = jnp.where(usable, cross, NONE_YET)
    best = jnp.max(cross.reshape(block // 8, 8, count), axis=0)
    tile = kept_ref.shape[0]
    for start in range(0, kept_ref.shape[0], tile):
        scores = lax.dot_general(
            kept_ref[start : start + tile, :], queries, contract, preferred_element_type=jnp.float32
        )
        best = jnp.maximum(best, jnp.max(scores.reshape(tile // 8, 8, count), axis=0))
    return jnp.max(best, axis=0, keepdims=True)


def flag_column(flag_ref):
    groups, count = flag_ref.shape
    row = lax.broadcasted_iota(jnp.int32, (count, count), 0)
    diagonal = row == lax.broadcasted_iota(jnp.int32, (count, count), 1)
    columns = []
    for n in range(groups):
        spread = jnp.broadcast_to(flag_ref[n : n + 1, :], (count, count))
        columns.append(jnp.sum(jnp.where(diagonal, spread, 0), axis=1, keepdims=True))
    return jnp.concatenate(columns, axis=0)


def gathered(refs, spans):
    return jnp.concatenate([r[a:b, :] for r, (a, b) in zip(refs, spans, strict=True)], axis=0)


def chunk_kernel(spans, micro_count, own_count, kept_ref, own_ref, flag_ref, *refs):
    parts = len(spans)
    queries = gathered(refs[:parts], spans)
    refs[parts][...] = best_of(kept_ref, own_ref, flag_ref, queries, micro_count, own_count)


def last_kernel(spans, masks, pair, micro_count, own_count, kept_ref, own_ref, flag_ref, *refs):
    parts = len(spans)
    queries = gathered(refs[:parts], spans)
    *earlier, out_ref = refs[parts:]
    block = micro_count * own_count
    me = lax.axis_index(AXES[0]) * lax.axis_size(AXES[1]) + lax.axis_index(AXES[1])
    second = jnp.bitwise_and(me, pair) != 0

    def place(best, owners):
        short = -best.shape[1] % LANES
        if short:
            best = jnp.concatenate([best, jnp.zeros((1, short), best.dtype)], axis=1)
        for at, (mask, other) in enumerate(owners):
            start = at * block
            base = start // LANES * LANES
            piece = best[:, base : base + LANES]
            if start - base:
                piece = pltpu.roll(piece, LANES - (start - base), 1)
            if other != mask:
                mask = jnp.where(second, other, mask)
            out_ref[jnp.bitwise_xor(me, mask)] = piece

    for ref, owners in zip(earlier, masks[:-1], strict=True):
        place(ref[...], owners)
    place(best_of(kept_ref, own_ref, flag_ref, queries, micro_count, own_count), masks[-1])


def pack(pieces, block):
    room = CHUNK_ROWS // block
    chunks, spans, owners = [], [], []
    for array, masks in pieces:
        at = 0
        while at < len(masks):
            take = min(room - len(owners), len(masks) - at)
            spans.append((array, at * block, (at + take) * block))
            owners += masks[at : at + take]
            at += take
            if len(owners) == room:
                chunks.append((spans, owners))
                spans, owners = [], []
    if owners:
        chunks.append((spans, owners))
    return chunks


def per_device(mesh, kept_slab, new_rows, append_mask):
    micro_count, own_count, width = new_rows.shape
    block = micro_count * own_count
    total = mesh.size
    pair, near, inner, outer = masks_of(mesh)
    own = new_rows.reshape(block, width)
    slab_rows = kept_slab.shape[0]
    vmem = pl.BlockSpec(memory_space=pltpu.VMEM)
    small = pltpu.CompilerParams(vmem_limit_bytes=8 * 2**20)
    large = pltpu.CompilerParams(vmem_limit_bytes=24 * 2**20)

    def join(*blocks):
        rows = sum(b.shape[0] for b in blocks)
        return pl.pallas_call(
            join_kernel,
            out_shape=jax.ShapeDtypeStruct((rows, width), own.dtype),
            in_specs=[vmem] * len(blocks),
            out_specs=vmem,
            compiler_params=small,
            cost_estimate=pl.CostEstimate(
                flops=JOIN_FLOPS, bytes_accessed=4 * rows * width, transcendentals=0
            ),
        )(*blocks)

    def chunk(spans, owners, bests=(), masks=()):
        rows = len(owners) * block
        cuts = [(a, b) for _, a, b in spans]
        best = jax.ShapeDtypeStruct((1, rows), jnp.float32)
        if masks:
            body = functools.partial(last_kernel, cuts, masks, pair)
            out = jax.ShapeDtypeStruct((total, 1, LANES), jnp.float32)
        else:
            body, out = functools.partial(chunk_kernel, cuts), best
        return pl.pallas_call(
            functools.partial(body, micro_count, own_count),
            out_shape=out,
            in_specs=[vmem] * (3 + len(spans) + len(bests)),
            out_specs=vmem,
            compiler_params=large,
            cost_estimate=pl.CostEstimate(
                flops=2 * rows * slab_rows * width,
                bytes_accessed=2 * slab_rows * width,
                transcendentals=0,
            ),
        )(kept_slab, own, append_mask, *[s[0] for s in spans], *bests)

    own_pair = swap(own, pair, total)
    z = [swap(own, m, total) for m in inner]
    twins = pl.pallas_call(
        twin_kernel,
        out_shape=jax.ShapeDtypeStruct((2 * block, width), own.dtype),
        in_specs=[pl.BlockSpec(memory_space=pltpu.HBM), vmem],
        out_specs=vmem,
        scratch_shapes=[pltpu.SemaphoreType.DMA(())],
        compiler_params=small,
    )(pltpu.with_memory_space_constraint(own, pltpu.HBM), own_pair)
    p = [swap(twins, outer[0], total, pair, outer[1])]
    p += [swap(own, m, total) for m in outer[2:]]
    line = join(*z)
    far = [swap(line, m, total) for m in outer]
    side = join(own, *p)
    beside = swap(side, near, total)
    first = join(side, line, far[0])
    first_pair = swap(first, pair, total)
    rest = join(*far[1:], beside)
    rest_pair = swap(rest, pair, total)

    both = lambda masks: [(m, m) for m in masks]
    across = lambda masks: [(b ^ pair, a ^ pair) for a, b in masks]
    planes = [(0, 0), (outer[0], outer[1]), (outer[0] ^ pair, outer[1] ^ pair), *both(outer[2:])]
    far_masks = [both([o ^ i for i in inner]) for o in outer]
    first_masks = planes + both(inner) + far_masks[0]
    rest_masks = sum(far_masks[1:], []) + [(a ^ near, b ^ near) for a, b in planes]
    pieces = [(first, first_masks), (first_pair, across(first_masks))]
    pieces += [(rest, rest_masks), (rest_pair, across(rest_masks))]
    chunks = pack(pieces, block)
    bests = [chunk(*c) for c in chunks[:-1]]
    partial = chunk(*chunks[-1], bests, [owners for _, owners in chunks])
    received = lax.all_to_all(partial, AXES, split_axis=0, concat_axis=0, tiled=True)
    return jnp.max(received[:, 0, :block], axis=0).reshape(micro_count, own_count)


def solution(mesh):
    def body(kept_slab, new_rows, append_mask):
        return per_device(mesh, kept_slab, new_rows, append_mask)

    return jax.shard_map(
        body,
        mesh=mesh,
        in_specs=(
            P(AXES, None),
            P(None, AXES, None),
            P(None, AXES),
        ),
        out_specs=P(None, AXES),
        check_vma=False,
    )
```
